256 devices in a mesh: dp: 32 (over z, y_hi, core), owner: 8 (over y_lo, x).
Axes of the slice: x: 4, y: 4 (y_hi: 2, y_lo: 2; y = y_hi * 2 + y_lo), z: 8, core: 2. Of those that a mesh axis runs over, the one named last changes fastest.
Arguments:
- inputs: bfloat16 [4096, 8192], P('dp'), may hold values from -12 to 12
- out_grads: bfloat16 [4096, 8192], P('dp', 'owner'), may hold values from -16 to 16
- weights: float32 [256, 512, 512], P(('dp', 'owner')), may hold values from -0.0625 to 0.0625
- left_stats: float32 [256, 512, 512], P(('dp', 'owner')), as said below
- right_stats: float32 [256, 512, 512], P(('dp', 'owner')), as said below
- left_roots: float32 [256, 512, 512], P(('dp', 'owner')), as said below
- right_roots: float32 [256, 512, 512], P(('dp', 'owner')), as said below
- refresh: int32 [256], P(('dp', 'owner')), may hold values from 0 to 1, as said below
Outputs:
- new_left_stats: float32 [256, 512, 512], P(('dp', 'owner'))
- new_right_stats: float32 [256, 512, 512], P(('dp', 'owner'))
- new_left_roots: float32 [256, 512, 512], P(('dp', 'owner'))
- new_right_roots: float32 [256, 512, 512], P(('dp', 'owner'))
- update: float32 [256, 512, 512], P(('dp', 'owner'))
- queries: bfloat16 [4096, 8192], P('dp', 'owner')
The draws below stay inside these ranges and needn't reach their ends.
Inputs may be any that keep to these rules, and one draw needn't show every extreme that they name: For every k, refresh[2k] + refresh[2k + 1] is at most 1, and refresh[0] + refresh[1] is 1. `left_stats`: every block is symmetric positive definite. `right_stats`: every block is symmetric positive definite. `left_roots`: every block is symmetric positive definite. `right_roots`: every block is symmetric positive definite.
All inputs are finite; a program needn't handle non-finite values.
Results may differ from the reference program's by a relative error of at most 0.015.
Values may be sent and summed in bfloat16 or wider, within the bound.
No kernel may reach another device: no remote copies, remote signals or barrier semaphores. Data moves between devices by JAX's collectives and lax.ppermute only.
A program may use at most 128 MiB of HBM per device.

```python
import math
import jax
import jax.numpy as jnp
from jax import lax

D = 8192
B = 512
NEWTON = 2
TOKENS = 4096
COL_DEV = 1024
COLS = 8192
BLOCKS = 256
N_DP = 32
N_OWNER = 8


def definite(key, count, order):
    keys = jax.random.split(key, 2)
    noise = jax.random.normal(keys[0], (count, order, order), jnp.float32) * (0.4 / order ** 0.5)
    noise = (noise + jnp.swapaxes(noise, 1, 2)) * 0.5 ** 0.5
    diagonal = jnp.exp(jax.random.uniform(keys[1], (count, order), jnp.float32, 0.0, 1.0986))
    identity = jnp.eye(order, dtype=jnp.float32)
    matrix = noise + diagonal[:, :, None] * identity[None, :, :]
    return matrix


def draw_left_stats(key, part):
    return definite(jax.random.fold_in(key, 11), BLOCKS, B)


def draw_right_stats(key, part):
    return definite(jax.random.fold_in(key, 12), BLOCKS, B)


def draw_left_roots(key, part):
    return definite(jax.random.fold_in(key, 13), BLOCKS, B)


def draw_right_roots(key, part):
    return definite(jax.random.fold_in(key, 14), BLOCKS, B)


def draw_refresh(key, part):
    pair_count = BLOCKS // 2
    keys = jax.random.split(jax.random.fold_in(key, 21), 2)
    active = (jax.random.randint(keys[0], (pair_count,), 0, 3) > 0).astype(jnp.int32)
    active = active.at[0].set(1)
    which_one = jax.random.randint(keys[1], (pair_count,), 0, 2)
    first_flag = active * (which_one == 0).astype(jnp.int32)
    second_flag = active - first_flag
    return jnp.stack([first_flag, second_flag], 1).reshape(BLOCKS)


def raised(entries, key, source, target, shards_of, factor):
    owner, partner = [(jnp.arange(entries.shape[position]) // (entries.shape[position] // shards_of)).reshape([-1 if axis == position else 1 for axis in range(entries.ndim)]) for position in (source, target)]
    chosen = jax.random.permutation(key, shards_of)[partner]
    strong = (owner == chosen) | (owner == (partner + shards_of // 2) % shards_of)
    return jnp.where(strong, factor * entries, entries)


def levels(own_key, shape, cuts, least, top_value):
    gain, own = 1.0, jax.random.fold_in(own_key, 6)
    for axis_at, shards_of in cuts:
        heights = jnp.exp(jax.random.uniform(jax.random.fold_in(own, axis_at), (shards_of,), jnp.float32, least / len(cuts), top_value / len(cuts)))
        gain = gain * jnp.repeat(heights, shape[axis_at] // shards_of).reshape([-1 if axis == axis_at else 1 for axis in range(len(shape))])
    return gain


def bell_draw(rng, extent, scale, bound, cuts=(), held_as=jnp.bfloat16):
    values = scale * jax.random.normal(rng, extent, jnp.float32)
    if cuts:
        values = values * levels(rng, extent, cuts, -0.22, 0.18)
    return jnp.clip(values, -bound, bound).astype(held_as)


def heavy_noise(rng, dims, scale, bound, shards, heavy, kind=jnp.bfloat16):
    drawn = scale * jax.random.normal(rng, dims, jnp.float32)
    if shards:
        drawn = drawn * levels(rng, dims, shards, -0.22, 0.18)
    return jnp.clip(raised(drawn, jax.random.fold_in(rng, 3), *heavy), -bound, bound).astype(kind)


def setup_inputs(seed: int = 0) -> dict:
    seeds = jax.random.split(jax.random.key(seed), 9)
    inputs = heavy_noise(seeds[0], (TOKENS, D), 1.0, 12.0, ((0, 32),), (0, 1, 32, 2.75))
    out_grads = bell_draw(seeds[1], (TOKENS, COLS), ((TOKENS / B) ** 0.5), 16.0, ((0, 32), (1, 8)))
    weights = bell_draw(seeds[2], (BLOCKS, B, B), D ** -0.5, 0.0625, ((0, 256),), jnp.float32)
    left_stats = draw_left_stats(jax.random.fold_in(seeds[8], 71), 0)
    right_stats = draw_right_stats(jax.random.fold_in(seeds[8], 71), 0)
    left_roots = draw_left_roots(jax.random.fold_in(seeds[8], 71), 0)
    right_roots = draw_right_roots(jax.random.fold_in(seeds[8], 71), 0)
    refresh = draw_refresh(jax.random.fold_in(seeds[8], 71), 0)
    return {"inputs": inputs, "out_grads": out_grads, "weights": weights, "left_stats": left_stats, "right_stats": right_stats, "left_roots": left_roots, "right_roots": right_roots, "refresh": refresh}


BETA = 0.95
DAMPING = 0.0001
HIGHEST = lax.Precision.HIGHEST

def matmul(left_mat, right_mat):
    return jnp.dot(left_mat, right_mat, precision=HIGHEST, preferred_element_type=jnp.float32)

def inverse_root(statistic):
    identity = jnp.eye(statistic.shape[0], dtype=jnp.float32)
    damped = statistic + DAMPING * identity
    factor_z = 2.5 / jnp.sqrt(jnp.sum(damped * damped))
    current = factor_z * damped
    result = jnp.sqrt(jnp.sqrt(factor_z)) * identity
    for turn in range(NEWTON):
        factor = 1.25 * identity - 0.25 * current
        result = matmul(result, factor)
        square = matmul(factor, factor)
        current = matmul(matmul(square, square), current)
    return result

def both_roots(left_stat, right_stat, left_old, right_old):
    return (inverse_root(left_stat), inverse_root(right_stat))

def stale_roots(left_stat, right_stat, left_old, right_old):
    return (left_old, right_old)

def reference(inputs, out_grads, weights, left_stats, right_stats, left_roots, right_roots, refresh):
    tok_total = inputs.shape[0]
    tok_local = tok_total // N_DP
    row_blocks = D // B
    col_blocks = COL_DEV // B
    x_parts = inputs.reshape(N_DP, tok_local, D)
    g_parts = out_grads.reshape(N_DP, tok_local, COLS)

    def add_part(running, pieces):
        x_piece, g_piece = pieces
        product = lax.dot_general(x_piece, g_piece, (((0,), (0,)), ((), ())), preferred_element_type=jnp.float32) / tok_total
        product = lax.optimization_barrier(product.astype(jnp.bfloat16))
        return (running + product.astype(jnp.float32), None)
    grad, unused = lax.scan(add_part, jnp.zeros((D, COLS), jnp.float32), (x_parts, g_parts))
    grad_blocks = grad.reshape(row_blocks, B, N_OWNER, col_blocks, B).transpose(0, 3, 2, 1, 4).reshape(BLOCKS, B, B)
    rate = 0.25 / math.sqrt(D)

    def per_block(items):
        grad_block, weight_block, left_stat, right_stat, left_old, right_old, flag_value = items
        left_new = BETA * left_stat + (1.0 - BETA) * matmul(grad_block, grad_block.T)
        right_new = BETA * right_stat + (1.0 - BETA) * matmul(grad_block.T, grad_block)
        left_root, right_root = lax.cond(flag_value > 0, both_roots, stale_roots, left_new, right_new, left_old, right_old)
        direction = matmul(matmul(left_root, grad_block), right_root)
        direction = direction * (B / jnp.sqrt(jnp.sum(direction * direction) + 1e-12))
        updated = (weight_block - rate * direction).astype(jnp.bfloat16)
        return (left_new, right_new, left_root, right_root, direction, updated)
    outputs = lax.map(per_block, (grad_blocks, weights, left_stats, right_stats, left_roots, right_roots, refresh))
    left_new, right_new, left_root, right_root, direction, updated = outputs
    full_weight = updated.reshape(row_blocks, col_blocks, N_OWNER, B, B).transpose(0, 3, 2, 1, 4).reshape(D, COLS)
    queries = jnp.dot(inputs, full_weight, preferred_element_type=jnp.float32).astype(jnp.bfloat16)
    return (left_new, right_new, left_root, right_root, direction, queries)
```

```python
import math

import jax
import jax.numpy as jnp
from jax import lax
from jax.experimental import pallas as pl
from jax.experimental.pallas import tpu as pltpu
from jax.sharding import Mesh
from jax.sharding import PartitionSpec as P

BETA = 0.95
DAMPING = 0.0001
FINE = ("z", "yh", "c", "yl", "x")
SIZES = (8, 2, 2, 2, 4)
NZ, NX = 8, 4
DP = ("z", "yh", "c")
OWNER = ("yl", "x")
F32 = jnp.float32
BF16 = jnp.bfloat16
VMEM = pl.BlockSpec(memory_space=pltpu.VMEM)
SMEM = pl.BlockSpec(memory_space=pltpu.SMEM)
RING = (0, -1, -2, -3, 1, 2, 3, 4)
ROW = (0, -1, 1, 2)


def shift(value, axis, step):
    size = SIZES[FINE.index(axis)]
    return lax.ppermute(value, axis, [(i, (i + step) % size) for i in range(size)])


def dot(a, b, dims=((1,), (0,))):
    return lax.dot_general(a, b, (dims, ((), ())), preferred_element_type=F32)


def gradient_kernel(place, *refs):
    own_x, other_x, parts = refs[0:4], refs[4:8], refs[8:17]
    keep, send, blocks = refs[17:20]
    z, x, yh = place[0], place[1], place[2]
    cots = jnp.concatenate([part[...] for part in parts], 0)
    for piece in range(NX):
        feats = []
        for step in RING:
            source = (z + step + NZ) % NZ
            feats += [own_x[piece][source], other_x[piece][source]]
        product = dot(jnp.concatenate(feats, 0), cots, ((0,), (0,)))
        blocks[(x + ROW[piece] + NX) % NX] = product * (1.0 / 4096)
    half = blocks.shape[1]
    for j in range(2):
        keep[pl.ds(j * half, half), :] = blocks[2 * yh + j]
        send[pl.ds(j * half, half), :] = blocks[2 * (1 - yh) + j].astype(BF16)


def eye_mask(order):
    rows = lax.broadcasted_iota(jnp.int32, (order, order), 0)
    cols = lax.broadcasted_iota(jnp.int32, (order, order), 1)
    return rows == cols


def root_of(stat):
    mask = eye_mask(stat.shape[0])
    damped = jnp.where(mask, stat + DAMPING, stat)
    scale = 2.5 / jnp.sqrt(jnp.sum(damped * damped, keepdims=True))
    start = scale * damped
    small = 0.25 * start
    small_b = small.astype(BF16)
    square = dot(small_b, small_b) - 2.5 * small
    square_b = square.astype(BF16)
    fourth = dot(square_b, square_b) + 3.125 * square
    moved = 2.44140625 * start + dot(fourth.astype(BF16), start.astype(BF16))
    small2 = 0.25 * moved
    result = dot(small_b, small2.astype(BF16)) - 1.25 * (small + small2)
    result = jnp.where(mask, result + 1.5625, result)
    return jnp.sqrt(jnp.sqrt(scale)) * result


def step_kernel(
    flag, keep, got, weights, left_stats, right_stats, left_roots, right_roots,
    left_new, right_new, left_root, right_root, update, updated,
):
    grad = keep[...] + got[...].astype(F32)
    grad_b = grad.astype(BF16)
    grad_t = grad_b.T
    left_new[...] = BETA * left_stats[...] + (1.0 - BETA) * dot(grad_b, grad_b, ((1,), (1,)))
    right_new[...] = BETA * right_stats[...] + (1.0 - BETA) * dot(grad_t, grad_t, ((1,), (1,)))

    @pl.when(flag[0] > 0)
    def _():
        left_root[...] = root_of(left_new[...])
        right_root[...] = root_of(right_new[...])

    @pl.when(flag[0] <= 0)
    def _():
        left_root[...] = left_roots[...]
        right_root[...] = right_roots[...]

    inner = dot(left_root[...].astype(BF16), grad_b).astype(BF16)
    direction = dot(inner, right_root[...].astype(BF16))
    total = jnp.sum(direction * direction, keepdims=True)
    direction = direction * (direction.shape[0] / jnp.sqrt(total + 1e-12))
    update[...] = direction
    updated[...] = (weights[...] - (0.25 / math.sqrt(8192)) * direction).astype(BF16)


def query_kernel(place, *refs):
    own_x, other_x = refs[0:4], refs[4:8]
    own_w, other_w, out, rows = refs[8:12]
    z, x, yh = place[0], place[1], place[2]
    half = rows.shape[1]
    for j in range(2):
        rows[2 * yh + j] = own_w[pl.ds(j * half, half), :]
        rows[2 * (1 - yh) + j] = other_w[pl.ds(j * half, half), :]
    weight = jnp.concatenate([rows[(x + step + NX) % NX] for step in ROW], 0)
    for k in range(NZ):
        target = (z + k) % NZ
        tokens = jnp.concatenate(
            [
                jnp.concatenate([piece[target] for piece in own_x], 1),
                jnp.concatenate([piece[target] for piece in other_x], 1),
            ],
            0,
        )
        out[k] = dot(tokens, weight).astype(BF16)


def call(kernel, out_shape, count, scratch=(), limit=32):
    return pl.pallas_call(
        kernel,
        out_shape=out_shape,
        in_specs=[SMEM] + [VMEM] * count,
        out_specs=jax.tree.map(lambda _: VMEM, out_shape),
        scratch_shapes=scratch,
        compiler_params=pltpu.CompilerParams(vmem_limit_bytes=limit * 1024 * 1024),
    )


def body(inputs, out_grads, weights, left_stats, right_stats, left_roots, right_roots, refresh):
    tokens, width = inputs.shape
    block = weights.shape[1]
    z, yh, core, x = (lax.axis_index(name) for name in ("z", "yh", "c", "x"))
    place = jnp.stack([z, x, yh]).astype(jnp.int32)

    low, high = out_grads[:, :block], out_grads[:, block:]
    mine = jnp.where(core == 0, low, high)
    theirs = jnp.where(core == 0, high, low)
    start = jnp.concatenate([mine, shift(theirs, "c", 1)], 0)
    up, down = [start], [start]
    for _ in range(3):
        up.append(shift(up[-1], "z", 1))
        down.append(shift(down[-1], "z", -1))
    far_low = shift(up[-1][:tokens], "z", 1)
    far_high = shift(down[-1][tokens:], "z", -1)
    cots = up + down[1:] + [far_low, far_high]

    quarter = width // (NZ * NX)
    split = inputs.reshape(tokens, NZ, NX, quarter)
    split = lax.dynamic_index_in_dim(split, x, 2, keepdims=False).transpose(1, 0, 2)
    split = lax.all_to_all(split, "z", 0, 0, tiled=True)
    own_x = [split, shift(split, "x", 1), shift(split, "x", -1), shift(split, "x", 2)]
    other_x = [shift(piece, "c", 1) for piece in own_x]

    square = (block, block)
    keep, send = call(
        gradient_kernel,
        (jax.ShapeDtypeStruct(square, F32), jax.ShapeDtypeStruct(square, BF16)),
        17,
        [pltpu.VMEM((NX, quarter, block), F32)],
    )(place, *own_x, *other_x, *cots)
    got = shift(send, "yh", 1)

    full = jax.ShapeDtypeStruct(square, F32)
    left_new, right_new, left_root, right_root, direction, updated = call(
        step_kernel, (full,) * 5 + (jax.ShapeDtypeStruct(square, BF16),), 7
    )(refresh, keep, got, weights[0], left_stats[0], right_stats[0], left_roots[0], right_roots[0])
    neighbour = shift(updated, "yh", 1)

    parts = call(
        query_kernel,
        jax.ShapeDtypeStruct((NZ, 2 * tokens, block), BF16),
        10,
        [pltpu.VMEM((NX, quarter, block), BF16)],
    )(place, *own_x, *other_x, updated, neighbour)

    near_up = shift(parts[1], "z", 1)
    near_down = shift(parts[7], "z", -1)
    up3 = shift(parts[3], "z", 1).astype(F32)
    down3 = shift(parts[5], "z", -1).astype(F32)
    up4 = shift(parts[4, :tokens], "z", 2).astype(F32)
    down4 = shift(parts[4, tokens:], "z", -2).astype(F32)
    up2 = parts[2].astype(F32) + up3
    up2 = jnp.concatenate([up2[:tokens] + up4, up2[tokens:]], 0).astype(BF16)
    down2 = parts[6].astype(F32) + down3
    down2 = jnp.concatenate([down2[:tokens], down2[tokens:] + down4], 0).astype(BF16)
    far_up = shift(up2, "z", 2)
    far_down = shift(down2, "z", -2)
    total = parts[0].astype(F32)
    for part in (near_up, near_down, far_up, far_down):
        total = total + part.astype(F32)
    total = total.astype(BF16)
    mine = total[:tokens]
    theirs = shift(total[tokens:], "c", 1)
    queries = jnp.concatenate(
        [jnp.where(core == 0, mine, theirs), jnp.where(core == 0, theirs, mine)], 1
    )
    return (
        left_new[None],
        right_new[None],
        left_root[None],
        right_root[None],
        direction[None],
        queries,
    )


def solution(mesh):
    fine = Mesh(mesh.devices.reshape(SIZES), FINE)
    blocks = P(DP + OWNER, None, None)
    in_specs = (P(DP, None), P(DP, OWNER)) + (blocks,) * 5 + (P(DP + OWNER),)
    out_specs = (blocks,) * 5 + (P(DP, OWNER),)
    return jax.shard_map(body, mesh=fine, in_specs=in_specs, out_specs=out_specs, check_vma=False)
```

```python
import math
from functools import partial

import jax
import jax.numpy as jnp
from jax import lax
from jax.experimental import pallas as pl
from jax.experimental.pallas import tpu as pltpu
from jax.sharding import Mesh
from jax.sharding import PartitionSpec as P

BETA = 0.95
DAMPING = 0.0001
FINE = ("z", "yh", "c", "yl", "x")
SIZES = (8, 2, 2, 2, 4)
NZ, NX = 8, 4
DP = ("z", "yh", "c")
OWNER = ("yl", "x")
F32 = jnp.float32
BF16 = jnp.bfloat16
VMEM = pl.BlockSpec(memory_space=pltpu.VMEM)
SMEM = pl.BlockSpec(memory_space=pltpu.SMEM)
ANY = pl.BlockSpec(memory_space=pl.ANY)
HBM = pl.BlockSpec(memory_space=pltpu.HBM)
RING = (0, -1, -2, -3, 1, 2, 3)
NEAR = (2, 6, 1, 7, 0)
ROW = (0, -1, 1, 2)


def shift(value, axis, step):
    size = SIZES[FINE.index(axis)]
    return lax.ppermute(value, axis, [(i, (i + step) % size) for i in range(size)])


def dot(a, b, dims=((1,), (0,))):
    return lax.dot_general(a, b, (dims, ((), ())), preferred_element_type=F32)


def tie(*values):
    return lax.optimization_barrier(values)


def feature_kernel(place, inputs, out, sems):
    x = place[1]
    copies = []
    for target in range(NZ):
        for j in range(2):
            column = pl.multiple_of((2 * target + j) * 512 + x * 128, 128)
            copy = pltpu.make_async_copy(
                inputs.at[:, pl.ds(column, 128)],
                out.at[target, :, pl.ds(j * 128, 128)],
                sems.at[2 * target + j],
            )
            copy.start()
            copies.append(copy)
    for copy in copies:
        copy.wait()


def copies_of(pairs, sems):
    copies = [
        pltpu.make_async_copy(source, target, sems.at[i]) for i, (source, target) in enumerate(pairs)
    ]
    for copy in copies:
        copy.start()
    return copies


def gradient_kernel(place, *refs):
    own_x, other_x, parts = refs[0:3], refs[3:6], refs[6:13]
    sums, feats, cots, sems = refs[13:17]
    z = place[0]
    pairs = [(part, cots.at[(z + step + NZ) % NZ]) for part, step in zip(parts, RING)]
    for piece in range(3):
        pairs.append((own_x[piece], feats.at[piece, :, 0]))
        pairs.append((other_x[piece], feats.at[piece, :, 1]))
    copies = copies_of(pairs, sems)
    cots[(z + 4) % NZ] = jnp.zeros(cots.shape[1:], BF16)
    for copy in copies[:7]:
        copy.wait()
    tokens = cots.shape[0] * cots.shape[1] * cots.shape[2]
    right = cots[...].reshape(tokens, cots.shape[3])
    for piece in range(3):
        copies[7 + 2 * piece].wait()
        copies[8 + 2 * piece].wait()
        left = feats[piece].reshape(tokens, feats.shape[4])
        sums[piece] = dot(left, right, ((0,), (0,)))


def put(total, yh, piece, keep, send):
    total = total * (1.0 / 4096)
    upper, lower = total[:128], total[128:]
    keep[piece] = jnp.where(yh == 0, upper, lower)
    send[piece] = jnp.where(yh == 0, lower, upper).astype(BF16)


def far_gradient_kernel(place, sums, feats, low, high, keep, send, cots, sems):
    copies = copies_of([(low, cots.at[0]), (high, cots.at[1])], sems)
    z, yh = place[0], place[2]
    for copy in copies:
        copy.wait()
    right = cots[...].reshape(256, cots.shape[2])
    for piece in range(3):
        left = feats[piece, (z + 4) % NZ].reshape(256, feats.shape[4])
        put(sums[piece] + dot(left, right, ((0,), (0,))), yh, piece, keep, send)


def last_gradient_kernel(place, own_r, own_l, other_r, other_l, cots, far, keep, send, feats, sems):
    half = NZ // 2
    copies = copies_of(
        [
            (own_r, feats.at[0, :half, 0]),
            (own_l, feats.at[0, half:, 0]),
            (other_r, feats.at[0, :half, 1]),
            (other_l, feats.at[0, half:, 1]),
        ],
        sems,
    )
    z, yh = place[0], place[2]
    tokens = cots.shape[0] * cots.shape[1] * cots.shape[2]
    for copy in copies:
        copy.wait()
    total = dot(
        feats[0].reshape(tokens, feats.shape[4]),
        cots[...].reshape(tokens, cots.shape[3]),
        ((0,), (0,)),
    )
    left = feats[0, (z + 4) % NZ].reshape(256, feats.shape[4])
    total = total + dot(left, far[...].reshape(256, far.shape[2]), ((0,), (0,)))
    put(total, yh, 0, keep, send)


def eye_mask(order):
    rows = lax.broadcasted_iota(jnp.int32, (order, order), 0)
    cols = lax.broadcasted_iota(jnp.int32, (order, order), 1)
    return rows == cols


def roots_of(stats):
    mask = eye_mask(stats[0].shape[0])
    damped = [jnp.where(mask, stat + DAMPING, stat) for stat in stats]
    scale = [2.5 / jnp.sqrt(jnp.sum(value * value, keepdims=True)) for value in damped]
    start = [a * b for a, b in zip(scale, damped)]
    start_b = [value.astype(BF16) for value in start]
    small = [0.25 * value for value in start]
    small_b = [value.astype(BF16) for value in small]
    square = [dot(b, b) - 2.5 * a for a, b in zip(small, small_b)]
    square_b = [value.astype(BF16) for value in square]
    fourth = [(dot(b, b) + 3.125 * a).astype(BF16) for a, b in zip(square, square_b)]
    moved = [2.44140625 * a + dot(c, b) for a, b, c in zip(start, start_b, fourth)]
    small2 = [0.25 * value for value in moved]
    small2_b = [value.astype(BF16) for value in small2]
    result = [
        dot(b, d) - 1.25 * (a + c) for a, b, c, d in zip(small, small_b, small2, small2_b)
    ]
    result = [jnp.where(mask, value + 1.5625, value) for value in result]
    return [jnp.sqrt(jnp.sqrt(a)) * b for a, b in zip(scale, result)]


def step_kernel(
    flag, place, keep3, keep1, got3, got1, weights, left_stats, right_stats, left_roots, right_roots,
    left_new, right_new, left_root, right_root, update, low_cols, high_cols, rows,
):
    x = place[1]
    for piece, step in enumerate(ROW):
        if piece < 3:
            value = keep3[piece] + got3[piece].astype(F32)
        else:
            value = keep1[0] + got1[0].astype(F32)
        rows[(x + step + NX) % NX] = value
    grad = rows[...].reshape(weights.shape)
    grad_b = grad.astype(BF16)
    grad_t = grad_b.T
    left_new[...] = BETA * left_stats[...] + (1.0 - BETA) * dot(grad_b, grad_b, ((1,), (1,)))
    right_new[...] = BETA * right_stats[...] + (1.0 - BETA) * dot(grad_t, grad_t, ((1,), (1,)))

    @pl.when(flag[0] > 0)
    def _():
        left_root[...], right_root[...] = roots_of((left_new[...], right_new[...]))

    @pl.when(flag[0] <= 0)
    def _():
        left_root[...] = left_roots[...]
        right_root[...] = right_roots[...]

    inner = dot(left_root[...].astype(BF16), grad_b).astype(BF16)
    direction = dot(inner, right_root[...].astype(BF16))
    total = jnp.sum(direction * direction, keepdims=True)
    direction = direction * (direction.shape[0] / jnp.sqrt(total + 1e-12))
    update[...] = direction
    updated = (weights[...] - (0.25 / math.sqrt(8192)) * direction).astype(BF16)
    low_cols[...] = updated[:, :256]
    high_cols[...] = updated[:, 256:]


def query_parts(place, feats3, feats1, own_w, other_w, rows):
    z, x, yh = place[0], place[1], place[2]
    for q in range(NX):
        rows[q, yh] = own_w[pl.ds(q * 128, 128), :]
        rows[q, 1 - yh] = other_w[pl.ds(q * 128, 128), :]
    weight = jnp.concatenate(
        [rows[(x + step + NX) % NX].reshape(256, rows.shape[3]) for step in ROW], 0
    )

    def part(k):
        target = (z + k) % NZ
        pieces = [feats3[piece, target] for piece in range(3)] + [feats1[0, target]]
        tokens = jnp.concatenate([piece.reshape(256, 256) for piece in pieces], 1)
        return dot(tokens, weight).astype(BF16)

    return part


def low_query_kernel(place, feats3, feats1, own_w, other_w, out, rows):
    part = query_parts(place, feats3, feats1, own_w, other_w, rows)
    for k in range(NZ):
        out[k] = part(k)


def high_query_kernel(
    place, feats3, feats1, own_w, other_w, low, up3, down3, up4, down4, up2, down2, up1, down1, here, rows
):
    part = query_parts(place, feats3, feats1, own_w, other_w, rows)
    for k, out in ((3, up3), (5, down3)):
        out[:, :256] = low[k]
        out[:, 256:] = part(k)
    both = part(4)
    up4[:, :256] = low[4, :128]
    up4[:, 256:] = both[:128]
    down4[:, :256] = low[4, 128:]
    down4[:, 256:] = both[128:]
    for k, out in zip(NEAR, (up2, down2, up1, down1, here)):
        out[:, :256] = low[k]
        out[:, 256:] = part(k)


def relay_kernel(half, mine, three, four, out):
    total = mine[...].astype(F32) + three[...].astype(F32)
    for i in range(2):
        value = total[i * 128 : i * 128 + 128]
        if i == half:
            value = value + four[...].astype(F32)
        out[pl.ds(i * 128, 128), :] = value.astype(BF16)


def call(kernel, out_shape, in_specs, out_specs=None, scratch=(), cost=None, limit=40):
    if out_specs is None:
        out_specs = jax.tree.map(lambda _: VMEM, out_shape)
    if cost is not None:
        cost = pl.CostEstimate(flops=cost[0], bytes_accessed=cost[1], transcendentals=0)
    return pl.pallas_call(
        kernel,
        out_shape=out_shape,
        in_specs=in_specs,
        out_specs=out_specs,
        scratch_shapes=scratch,
        cost_estimate=cost,
        compiler_params=pltpu.CompilerParams(vmem_limit_bytes=limit * 1024 * 1024),
    )


def body(inputs, out_grads, weights, left_stats, right_stats, left_roots, right_roots, refresh):
    tokens, width = inputs.shape
    block = weights.shape[1]
    z, yh, core, x = (lax.axis_index(name) for name in ("z", "yh", "c", "x"))
    place = jnp.stack([z, x, yh]).astype(jnp.int32)

    quarter = width // (NZ * NX)
    split = call(
        feature_kernel,
        jax.ShapeDtypeStruct((NZ, tokens, quarter), BF16),
        [SMEM, HBM],
        VMEM,
        [pltpu.SemaphoreType.DMA((2 * NZ,))],
    )(place, pltpu.with_memory_space_constraint(inputs, pltpu.HBM))

    low, high = out_grads[:, :block], out_grads[:, block:]
    mine = jnp.where(core == 0, low, high)
    theirs = jnp.where(core == 0, high, low)
    start = jnp.stack([mine, shift(theirs, "c", 1)], 0)
    up1, down1 = shift(start, "z", 1), shift(start, "z", -1)
    split = lax.all_to_all(split, "z", 0, 0, tiled=True)
    up1, down1, split = tie(up1, down1, split)
    right, left = shift(split, "x", 1), shift(split, "x", -1)
    other0 = shift(split, "c", 1)
    up2, down2 = shift(up1, "z", 1), shift(down1, "z", -1)
    up2, down2 = tie(up2, down2)
    up3, down3 = tie(shift(up2, "z", 1), shift(down2, "z", -1))
    far_low, far_high = shift(up3[0], "z", 1), shift(down3[1], "z", -1)
    other1, other2 = shift(right, "c", 1), shift(left, "c", 1)
    across_r = shift(right[: NZ // 2], "x", 1)
    across_l = shift(left[NZ // 2 :], "x", -1)

    feat_shape = (NZ, 2, tokens, quarter)
    cot_shape = (NZ, 2, tokens, block)
    sums, feats3, cots = call(
        gradient_kernel,
        (
            jax.ShapeDtypeStruct((3, quarter, block), F32),
            jax.ShapeDtypeStruct((3,) + feat_shape, BF16),
            jax.ShapeDtypeStruct(cot_shape, BF16),
        ),
        [SMEM] + [ANY] * 13,
        scratch=[pltpu.SemaphoreType.DMA((13,))],
        cost=(2 * NZ * 2 * tokens * 3 * quarter * block, 6 << 20),
    )(
        place, split, right, left, other0, other1, other2,
        start, up1, up2, up3, down1, down2, down3,
    )
    keep3, send3 = call(
        far_gradient_kernel,
        (
            jax.ShapeDtypeStruct((3, 128, block), F32),
            jax.ShapeDtypeStruct((3, 128, block), BF16),
        ),
        [SMEM, VMEM, VMEM, ANY, ANY],
        scratch=[pltpu.VMEM((2, tokens, block), BF16), pltpu.SemaphoreType.DMA((2,))],
    )(place, sums, feats3, far_low, far_high)
    keep3, across_r, across_l = tie(keep3, across_r, across_l)
    got3 = shift(send3, "yh", 1)
    far = jnp.stack([far_low, far_high], 0)
    keep1, send1, feats1 = call(
        last_gradient_kernel,
        (
            jax.ShapeDtypeStruct((1, 128, block), F32),
            jax.ShapeDtypeStruct((1, 128, block), BF16),
            jax.ShapeDtypeStruct((1,) + feat_shape, BF16),
        ),
        [SMEM] + [ANY] * 4 + [VMEM] * 2,
        scratch=[pltpu.SemaphoreType.DMA((4,))],
    )(place, across_r, across_l, shift(across_r, "c", 1), shift(across_l, "c", 1), cots, far)
    got1 = shift(send1, "yh", 1)

    square = (block, block)
    full = jax.ShapeDtypeStruct(square, F32)
    tall = jax.ShapeDtypeStruct((block, 256), BF16)
    left_new, right_new, left_root, right_root, direction, low_w, high_w = call(
        step_kernel,
        (full,) * 5 + (tall, tall),
        [SMEM, SMEM] + [VMEM] * 9,
        scratch=[pltpu.VMEM((NX, 128, block), F32)],
    )(
        refresh, place, keep3, keep1, got3, got1, weights[0],
        left_stats[0], right_stats[0], left_roots[0], right_roots[0],
    )
    low_got = shift(low_w, "yh", 1)
    high_got = shift(high_w, "yh", 1)

    half = jax.ShapeDtypeStruct((tokens, block), BF16)
    whole = jax.ShapeDtypeStruct((2 * tokens, block), BF16)
    rows = [pltpu.VMEM((NX, 2, 128, 256), BF16)]
    cost = (2 * NZ * 2 * tokens * NX * quarter * 256, 4 << 20)
    low_parts = call(
        low_query_kernel,
        jax.ShapeDtypeStruct((NZ, 2 * tokens, 256), BF16),
        [SMEM] + [VMEM] * 4,
        scratch=rows,
        cost=cost,
    )(place, feats3, feats1, low_w, low_got)
    up3, down3, up4, down4, up2, down2, up1, down1, here = call(
        high_query_kernel,
        (whole, whole, half, half) + (whole,) * 5,
        [SMEM] + [VMEM] * 5,
        scratch=rows,
        cost=cost,
    )(place, feats3, feats1, high_w, high_got, low_parts)
    up3, down3 = shift(up3, "z", 1), shift(down3, "z", -1)
    up4, down4 = shift(up4, "z", 2), shift(down4, "z", -2)
    up1, down1 = shift(up1, "z", 1), shift(down1, "z", -1)
    up2 = call(partial(relay_kernel, 0), whole, [VMEM] * 3)(up2, up3, up4)
    down2 = call(partial(relay_kernel, 1), whole, [VMEM] * 3)(down2, down3, down4)
    up2, down2 = shift(up2, "z", 2), shift(down2, "z", -2)
    total = here.astype(F32)
    for value in (up1, down1, up2, down2):
        total = total + value.astype(F32)
    total = total.astype(BF16)
    mine = total[:tokens]
    theirs = shift(total[tokens:], "c", 1)
    queries = jnp.concatenate(
        [jnp.where(core == 0, mine, theirs), jnp.where(core == 0, theirs, mine)], 1
    )
    return (
        left_new[None],
        right_new[None],
        left_root[None],
        right_root[None],
        direction[None],
        queries,
    )


def solution(mesh):
    fine = Mesh(mesh.devices.reshape(SIZES), FINE)
    blocks = P(DP + OWNER, None, None)
    in_specs = (P(DP, None), P(DP, OWNER)) + (blocks,) * 5 + (P(DP + OWNER),)
    out_specs = (blocks,) * 5 + (P(DP, OWNER),)
    return jax.shard_map(body, mesh=fine, in_specs=in_specs, out_specs=out_specs, check_vma=False)
```

```python
import math
from functools import partial

import jax
import jax.numpy as jnp
from jax import lax
from jax.experimental import pallas as pl
from jax.experimental.pallas import tpu as pltpu
from jax.sharding import Mesh
from jax.sharding import PartitionSpec as P

BETA = 0.95
DAMPING = 0.0001
FINE = ("z", "yh", "c", "yl", "x")
SIZES = (8, 2, 2, 2, 4)
NZ, NX = 8, 4
DP = ("z", "yh", "c")
OWNER = ("yl", "x")
F32 = jnp.float32
BF16 = jnp.bfloat16
VMEM = pl.BlockSpec(memory_space=pltpu.VMEM)
SMEM = pl.BlockSpec(memory_space=pltpu.SMEM)
ANY = pl.BlockSpec(memory_space=pl.ANY)
HBM = pl.BlockSpec(memory_space=pltpu.HBM)
RING = (0, -1, -2, -3, 1, 2, 3)
NEAR = (2, 6, 1, 7, 0)
ROW = (0, -1, 1, 2)


def shift(value, axis, step):
    size = SIZES[FINE.index(axis)]
    return lax.ppermute(value, axis, [(i, (i + step) % size) for i in range(size)])


def dot(a, b, dims=((1,), (0,))):
    return lax.dot_general(a, b, (dims, ((), ())), preferred_element_type=F32)


def tie(*values):
    return lax.optimization_barrier(values)


def feature_kernel(place, inputs, out, sems):
    x = place[1]
    copies = []
    for target in range(NZ):
        for j in range(2):
            column = pl.multiple_of((2 * target + j) * 512 + x * 128, 128)
            copy = pltpu.make_async_copy(
                inputs.at[:, pl.ds(column, 128)],
                out.at[target, :, pl.ds(j * 128, 128)],
                sems.at[2 * target + j],
            )
            copy.start()
            copies.append(copy)
    for copy in copies:
        copy.wait()


def copies_of(pairs, sems):
    copies = [
        pltpu.make_async_copy(source, target, sems.at[i]) for i, (source, target) in enumerate(pairs)
    ]
    for copy in copies:
        copy.start()
    return copies


def gradient_kernel(place, *refs):
    own_x, other_x, parts = refs[0:3], refs[3:6], refs[6:13]
    sums, feats, cots, sems = refs[13:17]
    z = place[0]
    pairs = [(part, cots.at[(z + step + NZ) % NZ]) for part, step in zip(parts, RING)]
    for piece in range(3):
        pairs.append((own_x[piece], feats.at[piece, :, 0]))
        pairs.append((other_x[piece], feats.at[piece, :, 1]))
    copies = copies_of(pairs, sems)
    cots[(z + 4) % NZ] = jnp.zeros(cots.shape[1:], BF16)
    for copy in copies[:7]:
        copy.wait()
    tokens = cots.shape[0] * cots.shape[1] * cots.shape[2]
    right = cots[...].reshape(tokens, cots.shape[3])
    for piece in range(3):
        copies[7 + 2 * piece].wait()
        copies[8 + 2 * piece].wait()
        left = feats[piece].reshape(tokens, feats.shape[4])
        sums[piece] = dot(left, right, ((0,), (0,)))


def put(total, yh, piece, keep, send):
    total = total * (1.0 / 4096)
    upper, lower = total[:128], total[128:]
    keep[piece] = jnp.where(yh == 0, upper, lower)
    send[piece] = jnp.where(yh == 0, lower, upper).astype(BF16)


def far_gradient_kernel(place, sums, feats, low, high, keep, send, cots, sems):
    copies = copies_of([(low, cots.at[0]), (high, cots.at[1])], sems)
    z, yh = place[0], place[2]
    for copy in copies:
        copy.wait()
    right = cots[...].reshape(256, cots.shape[2])
    for piece in range(3):
        left = feats[piece, (z + 4) % NZ].reshape(256, feats.shape[4])
        put(sums[piece] + dot(left, right, ((0,), (0,))), yh, piece, keep, send)


def last_gradient_kernel(place, own_r, own_l, other_r, other_l, cots, far, keep, send, feats, sems):
    half = NZ // 2
    copies = copies_of(
        [
            (own_r, feats.at[0, :half, 0]),
            (own_l, feats.at[0, half:, 0]),
            (other_r, feats.at[0, :half, 1]),
            (other_l, feats.at[0, half:, 1]),
        ],
        sems,
    )
    z, yh = place[0], place[2]
    tokens = cots.shape[0] * cots.shape[1] * cots.shape[2]
    for copy in copies:
        copy.wait()
    total = dot(
        feats[0].reshape(tokens, feats.shape[4]),
        cots[...].reshape(tokens, cots.shape[3]),
        ((0,), (0,)),
    )
    left = feats[0, (z + 4) % NZ].reshape(256, feats.shape[4])
    total = total + dot(left, far[...].reshape(256, far.shape[2]), ((0,), (0,)))
    put(total, yh, 0, keep, send)


def combine_kernel(keep, got, out):
    out[...] = keep[...] + got[...].astype(F32)


def eye_mask(order):
    rows = lax.broadcasted_iota(jnp.int32, (order, order), 0)
    cols = lax.broadcasted_iota(jnp.int32, (order, order), 1)
    return rows == cols


def roots_of(stats):
    mask = eye_mask(stats[0].shape[0])
    damped = [jnp.where(mask, stat + DAMPING, stat) for stat in stats]
    scale = [2.5 / jnp.sqrt(jnp.sum(value * value, keepdims=True)) for value in damped]
    start = [a * b for a, b in zip(scale, damped)]
    start_b = [value.astype(BF16) for value in start]
    small = [0.25 * value for value in start]
    small_b = [value.astype(BF16) for value in small]
    square = [dot(b, b) - 2.5 * a for a, b in zip(small, small_b)]
    square_b = [value.astype(BF16) for value in square]
    fourth = [(dot(b, b) + 3.125 * a).astype(BF16) for a, b in zip(square, square_b)]
    moved = [2.44140625 * a + dot(c, b) for a, b, c in zip(start, start_b, fourth)]
    small2 = [0.25 * value for value in moved]
    small2_b = [value.astype(BF16) for value in small2]
    result = [
        dot(b, d) - 1.25 * (a + c) for a, b, c, d in zip(small, small_b, small2, small2_b)
    ]
    result = [jnp.where(mask, value + 1.5625, value) for value in result]
    return [jnp.sqrt(jnp.sqrt(a)) * b for a, b in zip(scale, result)]


def step_kernel(
    flag, place, sum3, keep1, got1, weights, left_stats, right_stats, left_roots, right_roots,
    left_new, right_new, left_root, right_root, update, low_cols, high_cols, rows,
):
    x = place[1]
    for piece, step in enumerate(ROW):
        if piece < 3:
            value = sum3[piece]
        else:
            value = keep1[0] + got1[0].astype(F32)
        rows[(x + step + NX) % NX] = value
    grad = rows[...].reshape(weights.shape)
    grad_b = grad.astype(BF16)
    grad_t = grad_b.T
    left_new[...] = BETA * left_stats[...] + (1.0 - BETA) * dot(grad_b, grad_b, ((1,), (1,)))
    right_new[...] = BETA * right_stats[...] + (1.0 - BETA) * dot(grad_t, grad_t, ((1,), (1,)))

    @pl.when(flag[0] > 0)
    def _():
        left_root[...], right_root[...] = roots_of((left_new[...], right_new[...]))

    @pl.when(flag[0] <= 0)
    def _():
        left_root[...] = left_roots[...]
        right_root[...] = right_roots[...]

    inner = dot(left_root[...].astype(BF16), grad_b).astype(BF16)
    direction = dot(inner, right_root[...].astype(BF16))
    total = jnp.sum(direction * direction, keepdims=True)
    direction = direction * (direction.shape[0] / jnp.sqrt(total + 1e-12))
    update[...] = direction
    updated = (weights[...] - (0.25 / math.sqrt(8192)) * direction).astype(BF16)
    low_cols[...] = updated[:, :256]
    high_cols[...] = updated[:, 256:]


def query_parts(place, feats3, feats1, own_w, other_w, rows):
    z, x, yh = place[0], place[1], place[2]
    for q in range(NX):
        rows[q, yh] = own_w[pl.ds(q * 128, 128), :]
        rows[q, 1 - yh] = other_w[pl.ds(q * 128, 128), :]
    weight = jnp.concatenate(
        [rows[(x + step + NX) % NX].reshape(256, rows.shape[3]) for step in ROW], 0
    )

    def part(k):
        target = (z + k) % NZ
        pieces = [feats3[piece, target] for piece in range(3)] + [feats1[0, target]]
        tokens = jnp.concatenate([piece.reshape(256, 256) for piece in pieces], 1)
        return dot(tokens, weight).astype(BF16)

    return part


def low_query_kernel(place, feats3, feats1, own_w, other_w, out, rows):
    part = query_parts(place, feats3, feats1, own_w, other_w, rows)
    for k in range(NZ):
        out[k] = part(k)


def high_query_kernel(
    place, feats3, feats1, own_w, other_w, low, up3, down3, up4, down4, up2, down2, up1, down1, here, rows
):
    part = query_parts(place, feats3, feats1, own_w, other_w, rows)
    for k, out in ((3, up3), (5, down3)):
        out[:, :256] = low[k]
        out[:, 256:] = part(k)
    both = part(4)
    up4[:, :256] = low[4, :128]
    up4[:, 256:] = both[:128]
    down4[:, :256] = low[4, 128:]
    down4[:, 256:] = both[128:]
    for k, out in zip(NEAR, (up2, down2, up1, down1, here)):
        out[:, :256] = low[k]
        out[:, 256:] = part(k)


def relay_kernel(half, mine, three, four, out):
    total = mine[...].astype(F32) + three[...].astype(F32)
    for i in range(2):
        value = total[i * 128 : i * 128 + 128]
        if i == half:
            value = value + four[...].astype(F32)
        out[pl.ds(i * 128, 128), :] = value.astype(BF16)


def call(kernel, out_shape, in_specs, out_specs=None, scratch=(), cost=None, limit=40):
    if out_specs is None:
        out_specs = jax.tree.map(lambda _: VMEM, out_shape)
    if cost is not None:
        cost = pl.CostEstimate(flops=cost[0], bytes_accessed=cost[1], transcendentals=0)
    return pl.pallas_call(
        kernel,
        out_shape=out_shape,
        in_specs=in_specs,
        out_specs=out_specs,
        scratch_shapes=scratch,
        cost_estimate=cost,
        compiler_params=pltpu.CompilerParams(vmem_limit_bytes=limit * 1024 * 1024),
    )


def body(inputs, out_grads, weights, left_stats, right_stats, left_roots, right_roots, refresh):
    tokens, width = inputs.shape
    block = weights.shape[1]
    z, yh, core, x = (lax.axis_index(name) for name in ("z", "yh", "c", "x"))
    place = jnp.stack([z, x, yh]).astype(jnp.int32)

    quarter = width // (NZ * NX)
    split = call(
        feature_kernel,
        jax.ShapeDtypeStruct((NZ, tokens, quarter), BF16),
        [SMEM, HBM],
        VMEM,
        [pltpu.SemaphoreType.DMA((2 * NZ,))],
    )(place, pltpu.with_memory_space_constraint(inputs, pltpu.HBM))

    low, high = out_grads[:, :block], out_grads[:, block:]
    mine = jnp.where(core == 0, low, high)
    theirs = jnp.where(core == 0, high, low)
    start = jnp.stack([mine, shift(theirs, "c", 1)], 0)
    up1, down1 = shift(start, "z", 1), shift(start, "z", -1)
    split = lax.all_to_all(split, "z", 0, 0, tiled=True)
    up1, down1, split = tie(up1, down1, split)
    right, left = shift(split, "x", 1), shift(split, "x", -1)
    other0 = shift(split, "c", 1)
    up2, down2 = shift(up1, "z", 1), shift(down1, "z", -1)
    up2, down2 = tie(up2, down2)
    up3, down3 = tie(shift(up2, "z", 1), shift(down2, "z", -1))
    far_low, far_high = shift(up3[0], "z", 1), shift(down3[1], "z", -1)
    other1, other2 = shift(right, "c", 1), shift(left, "c", 1)
    right, left, other1, other2 = tie(right, left, other1, other2)
    across_r = shift(right[: NZ // 2], "x", 1)
    across_l = shift(left[NZ // 2 :], "x", -1)

    feat_shape = (NZ, 2, tokens, quarter)
    cot_shape = (NZ, 2, tokens, block)
    sums, feats3, cots = call(
        gradient_kernel,
        (
            jax.ShapeDtypeStruct((3, quarter, block), F32),
            jax.ShapeDtypeStruct((3,) + feat_shape, BF16),
            jax.ShapeDtypeStruct(cot_shape, BF16),
        ),
        [SMEM] + [ANY] * 13,
        scratch=[pltpu.SemaphoreType.DMA((13,))],
        cost=(2 * NZ * 2 * tokens * 3 * quarter * block * 8, 6 << 20),
    )(
        place, split, right, left, other0, other1, other2,
        start, up1, up2, up3, down1, down2, down3,
    )
    keep3, send3 = call(
        far_gradient_kernel,
        (
            jax.ShapeDtypeStruct((3, 128, block), F32),
            jax.ShapeDtypeStruct((3, 128, block), BF16),
        ),
        [SMEM, VMEM, VMEM, ANY, ANY],
        scratch=[pltpu.VMEM((2, tokens, block), BF16), pltpu.SemaphoreType.DMA((2,))],
    )(place, sums, feats3, far_low, far_high)
    keep3, across_r, across_l = tie(keep3, across_r, across_l)
    got3 = shift(send3, "yh", 1)
    far = jnp.stack([far_low, far_high], 0)
    keep1, send1, feats1 = call(
        last_gradient_kernel,
        (
            jax.ShapeDtypeStruct((1, 128, block), F32),
            jax.ShapeDtypeStruct((1, 128, block), BF16),
            jax.ShapeDtypeStruct((1,) + feat_shape, BF16),
        ),
        [SMEM] + [ANY] * 4 + [VMEM] * 2,
        scratch=[pltpu.SemaphoreType.DMA((4,))],
    )(place, across_r, across_l, shift(across_r, "c", 1), shift(across_l, "c", 1), cots, far)
    got1 = shift(send1, "yh", 1)

    sum3 = call(
        combine_kernel,
        jax.ShapeDtypeStruct((3, 128, block), F32),
        [VMEM, VMEM],
        cost=(1 << 34, 2 << 20),
    )(keep3, got3)

    square = (block, block)
    full = jax.ShapeDtypeStruct(square, F32)
    tall = jax.ShapeDtypeStruct((block, 256), BF16)
    left_new, right_new, left_root, right_root, direction, low_w, high_w = call(
        step_kernel,
        (full,) * 5 + (tall, tall),
        [SMEM, SMEM] + [VMEM] * 8,
        scratch=[pltpu.VMEM((NX, 128, block), F32)],
    )(
        refresh, place, sum3, keep1, got1, weights[0],
        left_stats[0], right_stats[0], left_roots[0], right_roots[0],
    )
    low_got = shift(low_w, "yh", 1)
    high_got = shift(high_w, "yh", 1)

    half = jax.ShapeDtypeStruct((tokens, block), BF16)
    whole = jax.ShapeDtypeStruct((2 * tokens, block), BF16)
    rows = [pltpu.VMEM((NX, 2, 128, 256), BF16)]
    cost = (2 * NZ * 2 * tokens * NX * quarter * 256, 4 << 20)
    low_parts = call(
        low_query_kernel,
        jax.ShapeDtypeStruct((NZ, 2 * tokens, 256), BF16),
        [SMEM] + [VMEM] * 4,
        scratch=rows,
        cost=cost,
    )(place, feats3, feats1, low_w, low_got)
    up3, down3, up4, down4, up2, down2, up1, down1, here = call(
        high_query_kernel,
        (whole, whole, half, half) + (whole,) * 5,
        [SMEM] + [VMEM] * 5,
        scratch=rows,
        cost=cost,
    )(place, feats3, feats1, high_w, high_got, low_parts)
    up3, down3 = shift(up3, "z", 1), shift(down3, "z", -1)
    up4, down4 = shift(up4, "z", 2), shift(down4, "z", -2)
    up1, down1 = shift(up1, "z", 1), shift(down1, "z", -1)
    up2 = call(partial(relay_kernel, 0), whole, [VMEM] * 3)(up2, up3, up4)
    down2 = call(partial(relay_kernel, 1), whole, [VMEM] * 3)(down2, down3, down4)
    up2, down2 = shift(up2, "z", 2), shift(down2, "z", -2)
    total = here.astype(F32)
    for value in (up1, down1, up2, down2):
        total = total + value.astype(F32)
    total = total.astype(BF16)
    mine = total[:tokens]
    theirs = shift(total[tokens:], "c", 1)
    queries = jnp.concatenate(
        [jnp.where(core == 0, mine, theirs), jnp.where(core == 0, theirs, mine)], 1
    )
    return (
        left_new[None],
        right_new[None],
        left_root[None],
        right_root[None],
        direction[None],
        queries,
    )


def solution(mesh):
    fine = Mesh(mesh.devices.reshape(SIZES), FINE)
    blocks = P(DP + OWNER, None, None)
    in_specs = (P(DP, None), P(DP, OWNER)) + (blocks,) * 5 + (P(DP + OWNER),)
    out_specs = (blocks,) * 5 + (P(DP, OWNER),)
    return jax.shard_map(body, mesh=fine, in_specs=in_specs, out_specs=out_specs, check_vma=False)
```

```python
import math
from functools import partial

import jax
import jax.numpy as jnp
from jax import lax
from jax.experimental import pallas as pl
from jax.experimental.pallas import tpu as pltpu
from jax.sharding import Mesh
from jax.sharding import PartitionSpec as P

BETA = 0.95
DAMPING = 0.0001
FINE = ("z", "yh", "c", "yl", "x")
SIZES = (8, 2, 2, 2, 4)
NZ, NX = 8, 4
DP = ("z", "yh", "c")
OWNER = ("yl", "x")
F32 = jnp.float32
BF16 = jnp.bfloat16
WIDE = 256
VMEM = pl.BlockSpec(memory_space=pltpu.VMEM)
SMEM = pl.BlockSpec(memory_space=pltpu.SMEM)
ANY = pl.BlockSpec(memory_space=pl.ANY)
HBM = pl.BlockSpec(memory_space=pltpu.HBM)
RING = (0, -1, -2, -3, 1, 2, 3)
NEAR = (2, 6, 1, 7, 0)
ROW = (0, -1, 1, 2)


def shift(value, axis, step):
    size = SIZES[FINE.index(axis)]
    return lax.ppermute(value, axis, [(i, (i + step) % size) for i in range(size)])


def dot(a, b, dims=((1,), (0,))):
    return lax.dot_general(a, b, (dims, ((), ())), preferred_element_type=F32)


def tie(*values):
    return lax.optimization_barrier(values)


def feature_kernel(place, inputs, out, sems):
    x = place[1]
    copies = []
    for target in range(NZ):
        for j in range(2):
            column = pl.multiple_of((2 * target + j) * 512 + x * 128, 128)
            copy = pltpu.make_async_copy(
                inputs.at[:, pl.ds(column, 128)],
                out.at[target, :, pl.ds(j * 128, 128)],
                sems.at[2 * target + j],
            )
            copy.start()
            copies.append(copy)
    for copy in copies:
        copy.wait()


def copies_of(pairs, sems):
    copies = [
        pltpu.make_async_copy(source, target, sems.at[i]) for i, (source, target) in enumerate(pairs)
    ]
    for copy in copies:
        copy.start()
    return copies


def gradient_kernel(place, *refs):
    own_x, other_x, parts = refs[0:3], refs[3:6], refs[6:13]
    sums, feats, cots, sems = refs[13:17]
    z = place[0]
    pairs = [(part, cots.at[(z + step + NZ) % NZ]) for part, step in zip(parts, RING)]
    for piece in range(3):
        pairs.append((own_x[piece], feats.at[piece, :, 0]))
        pairs.append((other_x[piece], feats.at[piece, :, 1]))
    copies = copies_of(pairs, sems)
    cots[(z + 4) % NZ] = jnp.zeros(cots.shape[1:], BF16)
    for copy in copies[:7]:
        copy.wait()
    tokens = cots.shape[0] * cots.shape[1] * cots.shape[2]
    right = cots[...].reshape(tokens, cots.shape[3])
    for piece in range(3):
        copies[7 + 2 * piece].wait()
        copies[8 + 2 * piece].wait()
        left = feats[piece].reshape(tokens, feats.shape[4])
        sums[piece] = dot(left, right, ((0,), (0,)))


def put(total, yh, piece, keep, send):
    total = total * (1.0 / 4096)
    upper, lower = total[:128], total[128:]
    keep[piece] = jnp.where(yh == 0, upper, lower)
    send[piece] = jnp.where(yh == 0, lower, upper).astype(BF16)


def far_gradient_kernel(place, sums, feats, low, high, keep, send, cots, sems):
    copies = copies_of([(low, cots.at[0]), (high, cots.at[1])], sems)
    z, yh = place[0], place[2]
    for copy in copies:
        copy.wait()
    right = cots[...].reshape(256, cots.shape[2])
    for piece in range(3):
        left = feats[piece, (z + 4) % NZ].reshape(256, feats.shape[4])
        put(sums[piece] + dot(left, right, ((0,), (0,))), yh, piece, keep, send)


def last_gradient_kernel(place, own_r, own_l, other_r, other_l, cots, far, keep, send, feats, sems):
    half = NZ // 2
    copies = copies_of(
        [
            (own_r, feats.at[0, :half, 0]),
            (own_l, feats.at[0, half:, 0]),
            (other_r, feats.at[0, :half, 1]),
            (other_l, feats.at[0, half:, 1]),
        ],
        sems,
    )
    z, yh = place[0], place[2]
    tokens = cots.shape[0] * cots.shape[1] * cots.shape[2]
    for copy in copies:
        copy.wait()
    total = dot(
        feats[0].reshape(tokens, feats.shape[4]),
        cots[...].reshape(tokens, cots.shape[3]),
        ((0,), (0,)),
    )
    left = feats[0, (z + 4) % NZ].reshape(256, feats.shape[4])
    total = total + dot(left, far[...].reshape(256, far.shape[2]), ((0,), (0,)))
    put(total, yh, 0, keep, send)


def combine_kernel(keep, got, out):
    out[...] = keep[...] + got[...].astype(F32)


def eye_mask(order):
    rows = lax.broadcasted_iota(jnp.int32, (order, order), 0)
    cols = lax.broadcasted_iota(jnp.int32, (order, order), 1)
    return rows == cols


def roots_of(stats):
    mask = eye_mask(stats[0].shape[0])
    damped = [jnp.where(mask, stat + DAMPING, stat) for stat in stats]
    scale = [2.5 / jnp.sqrt(jnp.sum(value * value, keepdims=True)) for value in damped]
    start = [a * b for a, b in zip(scale, damped)]
    start_b = [value.astype(BF16) for value in start]
    small = [0.25 * value for value in start]
    small_b = [value.astype(BF16) for value in small]
    square = [dot(b, b) - 2.5 * a for a, b in zip(small, small_b)]
    square_b = [value.astype(BF16) for value in square]
    fourth = [(dot(b, b) + 3.125 * a).astype(BF16) for a, b in zip(square, square_b)]
    moved = [2.44140625 * a + dot(c, b) for a, b, c in zip(start, start_b, fourth)]
    small2 = [0.25 * value for value in moved]
    small2_b = [value.astype(BF16) for value in small2]
    result = [
        dot(b, d) - 1.25 * (a + c) for a, b, c, d in zip(small, small_b, small2, small2_b)
    ]
    result = [jnp.where(mask, value + 1.5625, value) for value in result]
    return [jnp.sqrt(jnp.sqrt(a)) * b for a, b in zip(scale, result)]


def step_kernel(
    flag, place, sum3, keep1, got1, weights, left_stats, right_stats, left_roots, right_roots,
    left_new, right_new, left_root, right_root, update, low_cols, high_cols, rows,
):
    x = place[1]
    for piece, step in enumerate(ROW):
        if piece < 3:
            value = sum3[piece]
        else:
            value = keep1[0] + got1[0].astype(F32)
        rows[(x + step + NX) % NX] = value
    grad = rows[...].reshape(weights.shape)
    grad_b = grad.astype(BF16)
    grad_t = grad_b.T
    left_new[...] = BETA * left_stats[...] + (1.0 - BETA) * dot(grad_b, grad_b, ((1,), (1,)))
    right_new[...] = BETA * right_stats[...] + (1.0 - BETA) * dot(grad_t, grad_t, ((1,), (1,)))

    @pl.when(flag[0] > 0)
    def _():
        left_root[...], right_root[...] = roots_of((left_new[...], right_new[...]))

    @pl.when(flag[0] <= 0)
    def _():
        left_root[...] = left_roots[...]
        right_root[...] = right_roots[...]

    inner = dot(left_root[...].astype(BF16), grad_b).astype(BF16)
    direction = dot(inner, right_root[...].astype(BF16))
    total = jnp.sum(direction * direction, keepdims=True)
    direction = direction * (direction.shape[0] / jnp.sqrt(total + 1e-12))
    update[...] = direction
    updated = (weights[...] - (0.25 / math.sqrt(8192)) * direction).astype(BF16)
    low_cols[...] = updated[:, :WIDE]
    high_cols[...] = updated[:, WIDE:]


def query_parts(place, feats3, feats1, own_w, other_w, rows):
    z, x, yh = place[0], place[1], place[2]
    for q in range(NX):
        rows[q, yh] = own_w[pl.ds(q * 128, 128), :]
        rows[q, 1 - yh] = other_w[pl.ds(q * 128, 128), :]
    weight = jnp.concatenate(
        [rows[(x + step + NX) % NX].reshape(256, rows.shape[3]) for step in ROW], 0
    )

    def part(k):
        target = (z + k) % NZ
        pieces = [feats3[piece, target] for piece in range(3)] + [feats1[0, target]]
        tokens = jnp.concatenate([piece.reshape(256, 256) for piece in pieces], 1)
        return dot(tokens, weight).astype(BF16)

    return part


def low_query_kernel(place, feats3, feats1, own_w, other_w, out, rows):
    part = query_parts(place, feats3, feats1, own_w, other_w, rows)
    for k in range(NZ):
        out[k] = part(k)


def far_query_kernel(
    place, feats3, feats1, own_w, other_w, low, up3, down3, up4, down4, rows
):
    part = query_parts(place, feats3, feats1, own_w, other_w, rows)
    for k, out in ((3, up3), (5, down3)):
        out[:, :WIDE] = low[k]
        out[:, WIDE:] = part(k)
    both = part(4)
    up4[:, :WIDE] = low[4, :128]
    up4[:, WIDE:] = both[:128]
    down4[:, :WIDE] = low[4, 128:]
    down4[:, WIDE:] = both[128:]


def near_query_kernel(
    place, feats3, feats1, own_w, other_w, low, up2, down2, up1, down1, here, rows
):
    part = query_parts(place, feats3, feats1, own_w, other_w, rows)
    for k, out in zip(NEAR, (up2, down2, up1, down1, here)):
        out[:, :WIDE] = low[k]
        out[:, WIDE:] = part(k)


def relay_kernel(half, mine, three, four, out):
    total = mine[...].astype(F32) + three[...].astype(F32)
    for i in range(2):
        value = total[i * 128 : i * 128 + 128]
        if i == half:
            value = value + four[...].astype(F32)
        out[pl.ds(i * 128, 128), :] = value.astype(BF16)


def call(kernel, out_shape, in_specs, out_specs=None, scratch=(), cost=None, limit=40):
    if out_specs is None:
        out_specs = jax.tree.map(lambda _: VMEM, out_shape)
    if cost is not None:
        cost = pl.CostEstimate(flops=cost[0], bytes_accessed=cost[1], transcendentals=0)
    return pl.pallas_call(
        kernel,
        out_shape=out_shape,
        in_specs=in_specs,
        out_specs=out_specs,
        scratch_shapes=scratch,
        cost_estimate=cost,
        compiler_params=pltpu.CompilerParams(vmem_limit_bytes=limit * 1024 * 1024),
    )


def body(inputs, out_grads, weights, left_stats, right_stats, left_roots, right_roots, refresh):
    tokens, width = inputs.shape
    block = weights.shape[1]
    z, yh, core, x = (lax.axis_index(name) for name in ("z", "yh", "c", "x"))
    place = jnp.stack([z, x, yh]).astype(jnp.int32)

    quarter = width // (NZ * NX)
    split = call(
        feature_kernel,
        jax.ShapeDtypeStruct((NZ, tokens, quarter), BF16),
        [SMEM, HBM],
        VMEM,
        [pltpu.SemaphoreType.DMA((2 * NZ,))],
    )(place, pltpu.with_memory_space_constraint(inputs, pltpu.HBM))

    low, high = out_grads[:, :block], out_grads[:, block:]
    mine = jnp.where(core == 0, low, high)
    theirs = jnp.where(core == 0, high, low)
    start = jnp.stack([mine, shift(theirs, "c", 1)], 0)
    up1, down1 = shift(start, "z", 1), shift(start, "z", -1)
    split = lax.all_to_all(split, "z", 0, 0, tiled=True)
    up1, down1, split = tie(up1, down1, split)
    right, left = shift(split, "x", 1), shift(split, "x", -1)
    other0 = shift(split, "c", 1)
    up2, down2 = shift(up1, "z", 1), shift(down1, "z", -1)
    up2, down2 = tie(up2, down2)
    up3, down3 = tie(shift(up2, "z", 1), shift(down2, "z", -1))
    far_low, far_high = shift(up3[0], "z", 1), shift(down3[1], "z", -1)
    other1, other2 = shift(right, "c", 1), shift(left, "c", 1)
    right, left, other1, other2 = tie(right, left, other1, other2)
    across_r = shift(right[: NZ // 2], "x", 1)
    across_l = shift(left[NZ // 2 :], "x", -1)

    feat_shape = (NZ, 2, tokens, quarter)
    cot_shape = (NZ, 2, tokens, block)
    sums, feats3, cots = call(
        gradient_kernel,
        (
            jax.ShapeDtypeStruct((3, quarter, block), F32),
            jax.ShapeDtypeStruct((3,) + feat_shape, BF16),
            jax.ShapeDtypeStruct(cot_shape, BF16),
        ),
        [SMEM] + [ANY] * 13,
        scratch=[pltpu.SemaphoreType.DMA((13,))],
        cost=(2 * NZ * 2 * tokens * 3 * quarter * block * 8, 6 << 20),
    )(
        place, split, right, left, other0, other1, other2,
        start, up1, up2, up3, down1, down2, down3,
    )
    keep3, send3 = call(
        far_gradient_kernel,
        (
            jax.ShapeDtypeStruct((3, 128, block), F32),
            jax.ShapeDtypeStruct((3, 128, block), BF16),
        ),
        [SMEM, VMEM, VMEM, ANY, ANY],
        scratch=[pltpu.VMEM((2, tokens, block), BF16), pltpu.SemaphoreType.DMA((2,))],
    )(place, sums, feats3, far_low, far_high)
    keep3, across_r, across_l = tie(keep3, across_r, across_l)
    got3 = shift(send3, "yh", 1)
    far = jnp.stack([far_low, far_high], 0)
    keep1, send1, feats1 = call(
        last_gradient_kernel,
        (
            jax.ShapeDtypeStruct((1, 128, block), F32),
            jax.ShapeDtypeStruct((1, 128, block), BF16),
            jax.ShapeDtypeStruct((1,) + feat_shape, BF16),
        ),
        [SMEM] + [ANY] * 4 + [VMEM] * 2,
        scratch=[pltpu.SemaphoreType.DMA((4,))],
    )(place, across_r, across_l, shift(across_r, "c", 1), shift(across_l, "c", 1), cots, far)
    got1 = shift(send1, "yh", 1)

    sum3 = call(
        combine_kernel,
        jax.ShapeDtypeStruct((3, 128, block), F32),
        [VMEM, VMEM],
        cost=(1 << 34, 2 << 20),
    )(keep3, got3)

    square = (block, block)
    full = jax.ShapeDtypeStruct(square, F32)
    wide = jax.ShapeDtypeStruct((block, WIDE), BF16)
    narrow = jax.ShapeDtypeStruct((block, block - WIDE), BF16)
    left_new, right_new, left_root, right_root, direction, low_w, high_w = call(
        step_kernel,
        (full,) * 5 + (wide, narrow),
        [SMEM, SMEM] + [VMEM] * 8,
        scratch=[pltpu.VMEM((NX, 128, block), F32)],
    )(
        refresh, place, sum3, keep1, got1, weights[0],
        left_stats[0], right_stats[0], left_roots[0], right_roots[0],
    )
    low_got = shift(low_w, "yh", 1)
    high_got = shift(high_w, "yh", 1)

    half = jax.ShapeDtypeStruct((tokens, block), BF16)
    whole = jax.ShapeDtypeStruct((2 * tokens, block), BF16)
    low_parts = call(
        low_query_kernel,
        jax.ShapeDtypeStruct((NZ, 2 * tokens, WIDE), BF16),
        [SMEM] + [VMEM] * 4,
        scratch=[pltpu.VMEM((NX, 2, 128, WIDE), BF16)],
        cost=(1 << 31, 4 << 20),
    )(place, feats3, feats1, low_w, low_got)
    rows = [pltpu.VMEM((NX, 2, 128, block - WIDE), BF16)]
    operands = (place, feats3, feats1, high_w, high_got, low_parts)
    up3, down3, up4, down4 = call(
        far_query_kernel,
        (whole, whole, half, half),
        [SMEM] + [VMEM] * 5,
        scratch=rows,
        cost=(1 << 28, 2 << 20),
    )(*operands)
    up2, down2, up1, down1, here = call(
        near_query_kernel,
        (whole,) * 5,
        [SMEM] + [VMEM] * 5,
        scratch=rows,
        cost=(1 << 34, 2 << 20),
    )(*operands)
    up3, down3 = shift(up3, "z", 1), shift(down3, "z", -1)
    up4, down4 = shift(up4, "z", 2), shift(down4, "z", -2)
    up1, down1 = shift(up1, "z", 1), shift(down1, "z", -1)
    up2 = call(partial(relay_kernel, 0), whole, [VMEM] * 3)(up2, up3, up4)
    down2 = call(partial(relay_kernel, 1), whole, [VMEM] * 3)(down2, down3, down4)
    up2, down2 = shift(up2, "z", 2), shift(down2, "z", -2)
    total = here.astype(F32)
    for value in (up1, down1, up2, down2):
        total = total + value.astype(F32)
    total = total.astype(BF16)
    mine = total[:tokens]
    theirs = shift(total[tokens:], "c", 1)
    queries = jnp.concatenate(
        [jnp.where(core == 0, mine, theirs), jnp.where(core == 0, theirs, mine)], 1
    )
    return (
        left_new[None],
        right_new[None],
        left_root[None],
        right_root[None],
        direction[None],
        queries,
    )


def solution(mesh):
    fine = Mesh(mesh.devices.reshape(SIZES), FINE)
    blocks = P(DP + OWNER, None, None)
    in_specs = (P(DP, None), P(DP, OWNER)) + (blocks,) * 5 + (P(DP + OWNER),)
    out_specs = (blocks,) * 5 + (P(DP, OWNER),)
    return jax.shard_map(body, mesh=fine, in_specs=in_specs, out_specs=out_specs, check_vma=False)
```

```python
import math
from functools import partial

import jax
import jax.numpy as jnp
from jax import lax
from jax.experimental import pallas as pl
from jax.experimental.pallas import tpu as pltpu
from jax.sharding import Mesh
from jax.sharding import PartitionSpec as P

BETA = 0.95
DAMPING = 0.0001
FINE = ("z", "yh", "c", "yl", "x")
SIZES = (8, 2, 2, 2, 4)
NZ, NX = 8, 4
DP = ("z", "yh", "c")
OWNER = ("yl", "x")
F32 = jnp.float32
BF16 = jnp.bfloat16
WIDE = 256
VMEM = pl.BlockSpec(memory_space=pltpu.VMEM)
SMEM = pl.BlockSpec(memory_space=pltpu.SMEM)
ANY = pl.BlockSpec(memory_space=pl.ANY)
HBM = pl.BlockSpec(memory_space=pltpu.HBM)
RING = (0, -1, -2, -3, 1, 2, 3)
NEAR = (2, 6, 1, 7, 0)
ROW = (0, -1, 1, 2)


def shift(value, axis, step):
    size = SIZES[FINE.index(axis)]
    return lax.ppermute(value, axis, [(i, (i + step) % size) for i in range(size)])


def dot(a, b, dims=((1,), (0,))):
    return lax.dot_general(a, b, (dims, ((), ())), preferred_element_type=F32)


def tie(*values):
    return lax.optimization_barrier(values)


def feature_kernel(place, inputs, out, sems):
    x = place[1]
    copies = []
    for target in range(NZ):
        for j in range(2):
            column = pl.multiple_of((2 * target + j) * 512 + x * 128, 128)
            copy = pltpu.make_async_copy(
                inputs.at[:, pl.ds(column, 128)],
                out.at[target, :, pl.ds(j * 128, 128)],
                sems.at[2 * target + j],
            )
            copy.start()
            copies.append(copy)
    for copy in copies:
        copy.wait()


def copies_of(pairs, sems):
    copies = [
        pltpu.make_async_copy(source, target, sems.at[i]) for i, (source, target) in enumerate(pairs)
    ]
    for copy in copies:
        copy.start()
    return copies


def gradient_kernel(place, *refs):
    own_x, other_x, parts = refs[0:3], refs[3:6], refs[6:13]
    sums, feats, cots, sems = refs[13:17]
    z = place[0]
    pairs = [(part, cots.at[(z + step + NZ) % NZ]) for part, step in zip(parts, RING)]
    for piece in range(3):
        pairs.append((own_x[piece], feats.at[piece, :, 0]))
        pairs.append((other_x[piece], feats.at[piece, :, 1]))
    copies = copies_of(pairs, sems)
    cots[(z + 4) % NZ] = jnp.zeros(cots.shape[1:], BF16)
    for copy in copies[:7]:
        copy.wait()
    tokens = cots.shape[0] * cots.shape[1] * cots.shape[2]
    right = cots[...].reshape(tokens, cots.shape[3])
    for piece in range(3):
        copies[7 + 2 * piece].wait()
        copies[8 + 2 * piece].wait()
        left = feats[piece].reshape(tokens, feats.shape[4])
        sums[piece] = dot(left, right, ((0,), (0,)))


def forward_kernel(up, down, up_out, down_out):
    up_out[...] = up[...]
    down_out[...] = down[...]


def put(total, yh, piece, keep, send):
    total = total * (1.0 / 4096)
    upper, lower = total[:128], total[128:]
    keep[piece] = jnp.where(yh == 0, upper, lower)
    send[piece] = jnp.where(yh == 0, lower, upper).astype(BF16)


def far_gradient_kernel(place, sums, feats, low, high, keep, send, cots, sems):
    copies = copies_of([(low, cots.at[0]), (high, cots.at[1])], sems)
    z, yh = place[0], place[2]
    for copy in copies:
        copy.wait()
    right = cots[...].reshape(256, cots.shape[2])
    for piece in range(3):
        left = feats[piece, (z + 4) % NZ].reshape(256, feats.shape[4])
        put(sums[piece] + dot(left, right, ((0,), (0,))), yh, piece, keep, send)


def last_gradient_kernel(place, own_r, own_l, other_r, other_l, cots, far, keep, send, feats, sems):
    half = NZ // 2
    copies = copies_of(
        [
            (own_r, feats.at[0, :half, 0]),
            (own_l, feats.at[0, half:, 0]),
            (other_r, feats.at[0, :half, 1]),
            (other_l, feats.at[0, half:, 1]),
        ],
        sems,
    )
    z, yh = place[0], place[2]
    tokens = cots.shape[0] * cots.shape[1] * cots.shape[2]
    for copy in copies:
        copy.wait()
    total = dot(
        feats[0].reshape(tokens, feats.shape[4]),
        cots[...].reshape(tokens, cots.shape[3]),
        ((0,), (0,)),
    )
    left = feats[0, (z + 4) % NZ].reshape(256, feats.shape[4])
    total = total + dot(left, far[...].reshape(256, far.shape[2]), ((0,), (0,)))
    put(total, yh, 0, keep, send)


def combine_kernel(keep, got, out):
    out[...] = keep[...] + got[...].astype(F32)


def eye_mask(order):
    rows = lax.broadcasted_iota(jnp.int32, (order, order), 0)
    cols = lax.broadcasted_iota(jnp.int32, (order, order), 1)
    return rows == cols


def roots_of(stats):
    mask = eye_mask(stats[0].shape[0])
    damped = [jnp.where(mask, stat + DAMPING, stat) for stat in stats]
    scale = [2.5 / jnp.sqrt(jnp.sum(value * value, keepdims=True)) for value in damped]
    start = [a * b for a, b in zip(scale, damped)]
    start_b = [value.astype(BF16) for value in start]
    small = [0.25 * value for value in start]
    small_b = [value.astype(BF16) for value in small]
    square = [dot(b, b) - 2.5 * a for a, b in zip(small, small_b)]
    square_b = [value.astype(BF16) for value in square]
    fourth = [(dot(b, b) + 3.125 * a).astype(BF16) for a, b in zip(square, square_b)]
    moved = [2.44140625 * a + dot(c, b) for a, b, c in zip(start, start_b, fourth)]
    small2 = [0.25 * value for value in moved]
    small2_b = [value.astype(BF16) for value in small2]
    result = [
        dot(b, d) - 1.25 * (a + c) for a, b, c, d in zip(small, small_b, small2, small2_b)
    ]
    result = [jnp.where(mask, value + 1.5625, value) for value in result]
    return [jnp.sqrt(jnp.sqrt(a)) * b for a, b in zip(scale, result)]


def step_kernel(
    flag, place, sum3, keep1, got1, weights, left_stats, right_stats, left_roots, right_roots,
    left_new, right_new, left_root, right_root, update, low_cols, high_cols, rows,
):
    x = place[1]
    for piece, step in enumerate(ROW):
        if piece < 3:
            value = sum3[piece]
        else:
            value = keep1[0] + got1[0].astype(F32)
        rows[(x + step + NX) % NX] = value
    grad = rows[...].reshape(weights.shape)
    grad_b = grad.astype(BF16)
    grad_t = grad_b.T
    left_new[...] = BETA * left_stats[...] + (1.0 - BETA) * dot(grad_b, grad_b, ((1,), (1,)))
    right_new[...] = BETA * right_stats[...] + (1.0 - BETA) * dot(grad_t, grad_t, ((1,), (1,)))

    @pl.when(flag[0] > 0)
    def _():
        left_root[...], right_root[...] = roots_of((left_new[...], right_new[...]))

    @pl.when(flag[0] <= 0)
    def _():
        left_root[...] = left_roots[...]
        right_root[...] = right_roots[...]

    inner = dot(left_root[...].astype(BF16), grad_b).astype(BF16)
    direction = dot(inner, right_root[...].astype(BF16))
    total = jnp.sum(direction * direction, keepdims=True)
    direction = direction * (direction.shape[0] / jnp.sqrt(total + 1e-12))
    update[...] = direction
    updated = (weights[...] - (0.25 / math.sqrt(8192)) * direction).astype(BF16)
    low_cols[...] = updated[:, :WIDE]
    high_cols[...] = updated[:, WIDE:]


def query_parts(place, feats3, feats1, own_w, other_w, rows):
    z, x, yh = place[0], place[1], place[2]
    for q in range(NX):
        rows[q, yh] = own_w[pl.ds(q * 128, 128), :]
        rows[q, 1 - yh] = other_w[pl.ds(q * 128, 128), :]
    weight = jnp.concatenate(
        [rows[(x + step + NX) % NX].reshape(256, rows.shape[3]) for step in ROW], 0
    )

    def part(k):
        target = (z + k) % NZ
        pieces = [feats3[piece, target] for piece in range(3)] + [feats1[0, target]]
        tokens = jnp.concatenate([piece.reshape(256, 256) for piece in pieces], 1)
        return dot(tokens, weight).astype(BF16)

    return part


def low_query_kernel(place, feats3, feats1, own_w, other_w, out, rows):
    part = query_parts(place, feats3, feats1, own_w, other_w, rows)
    for k in range(NZ):
        out[k] = part(k)


def far_query_kernel(
    place, feats3, feats1, own_w, other_w, low, up3, down3, up4, down4, rows
):
    part = query_parts(place, feats3, feats1, own_w, other_w, rows)
    for k, out in ((3, up3), (5, down3)):
        out[:, :WIDE] = low[k]
        out[:, WIDE:] = part(k)
    both = part(4)
    up4[:, :WIDE] = low[4, :128]
    up4[:, WIDE:] = both[:128]
    down4[:, :WIDE] = low[4, 128:]
    down4[:, WIDE:] = both[128:]


def near_query_kernel(
    place, feats3, feats1, own_w, other_w, low, up2, down2, up1, down1, here, rows
):
    part = query_parts(place, feats3, feats1, own_w, other_w, rows)
    for k, out in zip(NEAR, (up2, down2, up1, down1, here)):
        out[:, :WIDE] = low[k]
        out[:, WIDE:] = part(k)


def relay_kernel(half, mine, three, four, out):
    total = mine[...].astype(F32) + three[...].astype(F32)
    for i in range(2):
        value = total[i * 128 : i * 128 + 128]
        if i == half:
            value = value + four[...].astype(F32)
        out[pl.ds(i * 128, 128), :] = value.astype(BF16)


def call(kernel, out_shape, in_specs, out_specs=None, scratch=(), cost=None, limit=40):
    if out_specs is None:
        out_specs = jax.tree.map(lambda _: VMEM, out_shape)
    if cost is not None:
        cost = pl.CostEstimate(flops=cost[0], bytes_accessed=cost[1], transcendentals=0)
    return pl.pallas_call(
        kernel,
        out_shape=out_shape,
        in_specs=in_specs,
        out_specs=out_specs,
        scratch_shapes=scratch,
        cost_estimate=cost,
        compiler_params=pltpu.CompilerParams(vmem_limit_bytes=limit * 1024 * 1024),
    )


def body(inputs, out_grads, weights, left_stats, right_stats, left_roots, right_roots, refresh):
    tokens, width = inputs.shape
    block = weights.shape[1]
    z, yh, core, x = (lax.axis_index(name) for name in ("z", "yh", "c", "x"))
    place = jnp.stack([z, x, yh]).astype(jnp.int32)

    quarter = width // (NZ * NX)
    split = call(
        feature_kernel,
        jax.ShapeDtypeStruct((NZ, tokens, quarter), BF16),
        [SMEM, HBM],
        VMEM,
        [pltpu.SemaphoreType.DMA((2 * NZ,))],
    )(place, pltpu.with_memory_space_constraint(inputs, pltpu.HBM))

    low, high = out_grads[:, :block], out_grads[:, block:]
    mine = jnp.where(core == 0, low, high)
    theirs = jnp.where(core == 0, high, low)
    start = jnp.stack([mine, shift(theirs, "c", 1)], 0)
    up1, down1 = shift(start, "z", 1), shift(start, "z", -1)
    split = lax.all_to_all(split, "z", 0, 0, tiled=True)
    up1, down1, split = tie(up1, down1, split)
    right, left = shift(split, "x", 1), shift(split, "x", -1)
    other0 = shift(split, "c", 1)
    up2, down2 = shift(up1, "z", 1), shift(down1, "z", -1)
    up2, down2 = tie(up2, down2)
    step = jax.ShapeDtypeStruct((2, tokens, block), BF16)
    up2, down2 = call(forward_kernel, (step, step), [VMEM, VMEM], cost=(1 << 31, 2 << 20))(up2, down2)
    up3, down3 = tie(shift(up2, "z", 1), shift(down2, "z", -1))
    far_low, far_high = shift(up3[0], "z", 1), shift(down3[1], "z", -1)
    other1, other2 = shift(right, "c", 1), shift(left, "c", 1)
    right, left, other1, other2 = tie(right, left, other1, other2)
    across_r = shift(right[: NZ // 2], "x", 1)
    across_l = shift(left[NZ // 2 :], "x", -1)

    feat_shape = (NZ, 2, tokens, quarter)
    cot_shape = (NZ, 2, tokens, block)
    sums, feats3, cots = call(
        gradient_kernel,
        (
            jax.ShapeDtypeStruct((3, quarter, block), F32),
            jax.ShapeDtypeStruct((3,) + feat_shape, BF16),
            jax.ShapeDtypeStruct(cot_shape, BF16),
        ),
        [SMEM] + [ANY] * 13,
        scratch=[pltpu.SemaphoreType.DMA((13,))],
        cost=(2 * NZ * 2 * tokens * 3 * quarter * block * 8, 6 << 20),
    )(
        place, split, right, left, other0, other1, other2,
        start, up1, up2, up3, down1, down2, down3,
    )
    keep3, send3 = call(
        far_gradient_kernel,
        (
            jax.ShapeDtypeStruct((3, 128, block), F32),
            jax.ShapeDtypeStruct((3, 128, block), BF16),
        ),
        [SMEM, VMEM, VMEM, ANY, ANY],
        scratch=[pltpu.VMEM((2, tokens, block), BF16), pltpu.SemaphoreType.DMA((2,))],
    )(place, sums, feats3, far_low, far_high)
    keep3, across_r, across_l = tie(keep3, across_r, across_l)
    got3 = shift(send3, "yh", 1)
    far = jnp.stack([far_low, far_high], 0)
    keep1, send1, feats1 = call(
        last_gradient_kernel,
        (
            jax.ShapeDtypeStruct((1, 128, block), F32),
            jax.ShapeDtypeStruct((1, 128, block), BF16),
            jax.ShapeDtypeStruct((1,) + feat_shape, BF16),
        ),
        [SMEM] + [ANY] * 4 + [VMEM] * 2,
        scratch=[pltpu.SemaphoreType.DMA((4,))],
    )(place, across_r, across_l, shift(across_r, "c", 1), shift(across_l, "c", 1), cots, far)
    got1 = shift(send1, "yh", 1)

    sum3 = call(
        combine_kernel,
        jax.ShapeDtypeStruct((3, 128, block), F32),
        [VMEM, VMEM],
        cost=(1 << 34, 2 << 20),
    )(keep3, got3)

    square = (block, block)
    full = jax.ShapeDtypeStruct(square, F32)
    wide = jax.ShapeDtypeStruct((block, WIDE), BF16)
    narrow = jax.ShapeDtypeStruct((block, block - WIDE), BF16)
    left_new, right_new, left_root, right_root, direction, low_w, high_w = call(
        step_kernel,
        (full,) * 5 + (wide, narrow),
        [SMEM, SMEM] + [VMEM] * 8,
        scratch=[pltpu.VMEM((NX, 128, block), F32)],
    )(
        refresh, place, sum3, keep1, got1, weights[0],
        left_stats[0], right_stats[0], left_roots[0], right_roots[0],
    )
    low_got = shift(low_w, "yh", 1)
    high_got = shift(high_w, "yh", 1)

    half = jax.ShapeDtypeStruct((tokens, block), BF16)
    whole = jax.ShapeDtypeStruct((2 * tokens, block), BF16)
    low_parts = call(
        low_query_kernel,
        jax.ShapeDtypeStruct((NZ, 2 * tokens, WIDE), BF16),
        [SMEM] + [VMEM] * 4,
        scratch=[pltpu.VMEM((NX, 2, 128, WIDE), BF16)],
        cost=(1 << 31, 4 << 20),
    )(place, feats3, feats1, low_w, low_got)
    rows = [pltpu.VMEM((NX, 2, 128, block - WIDE), BF16)]
    operands = (place, feats3, feats1, high_w, high_got, low_parts)
    up3, down3, up4, down4 = call(
        far_query_kernel,
        (whole, whole, half, half),
        [SMEM] + [VMEM] * 5,
        scratch=rows,
        cost=(1 << 28, 2 << 20),
    )(*operands)
    up2, down2, up1, down1, here = call(
        near_query_kernel,
        (whole,) * 5,
        [SMEM] + [VMEM] * 5,
        scratch=rows,
        cost=(1 << 34, 2 << 20),
    )(*operands)
    up3, down3 = shift(up3, "z", 1), shift(down3, "z", -1)
    up4, down4 = shift(up4, "z", 2), shift(down4, "z", -2)
    up1, down1 = shift(up1, "z", 1), shift(down1, "z", -1)
    up2 = call(partial(relay_kernel, 0), whole, [VMEM] * 3)(up2, up3, up4)
    down2 = call(partial(relay_kernel, 1), whole, [VMEM] * 3)(down2, down3, down4)
    up2, down2 = shift(up2, "z", 2), shift(down2, "z", -2)
    total = here.astype(F32)
    for value in (up1, down1, up2, down2):
        total = total + value.astype(F32)
    total = total.astype(BF16)
    mine = total[:tokens]
    theirs = shift(total[tokens:], "c", 1)
    queries = jnp.concatenate(
        [jnp.where(core == 0, mine, theirs), jnp.where(core == 0, theirs, mine)], 1
    )
    return (
        left_new[None],
        right_new[None],
        left_root[None],
        right_root[None],
        direction[None],
        queries,
    )


def solution(mesh):
    fine = Mesh(mesh.devices.reshape(SIZES), FINE)
    blocks = P(DP + OWNER, None, None)
    in_specs = (P(DP, None), P(DP, OWNER)) + (blocks,) * 5 + (P(DP + OWNER),)
    out_specs = (blocks,) * 5 + (P(DP, OWNER),)
    return jax.shard_map(body, mesh=fine, in_specs=in_specs, out_specs=out_specs, check_vma=False)
```
